512 devices in a mesh: layer: 16 (over z, core), ex: 32 (over y, x).
Axes of the slice: x: 4, y: 8, z: 8, core: 2. Of those that a mesh axis runs over, the one named last changes fastest.
Arguments:
- train_grads: bfloat16 [16384, 16, 4096], P('ex', 'layer'), may hold values from -0.3984375 to 0.3984375
- query_grads: bfloat16 [2048, 16, 4096], P('ex', 'layer'), may hold values from -0.3984375 to 0.3984375
- in_precond: float32 [16, 64, 64], P('layer'), as said below
- out_precond: float32 [16, 64, 64], P('layer'), as said below
- pair_blocks: int32 [768], replicated, may hold values from -1 to 127, as said below
Outputs:
- tile_out: float32 [16, 768, 512], P('layer', 'ex')
The draws below stay inside these ranges and needn't reach their ends.
Inputs may be any that keep to these rules, and one draw needn't show every extreme that they name: `pair_blocks`: slots p of training block p // 24 name query blocks (query block q holds judged examples q * 16 to q * 16 + 15 and lies on ex index q // 4), or -1 for an empty slot; the blocks named by one training block lie on distinct ex indices; empty slots come after filled ones; every training block fills at least 6 slots and some training block fills all 24. `in_precond`: each layer's factor is symmetric positive definite. `out_precond`: each layer's factor is symmetric positive definite.
All inputs are finite; a program needn't handle non-finite values.
Results may differ from the reference program's by a relative error of at most 0.0029.
Values may be sent and summed in bfloat16 or wider, within the bound.
A program may use at most 64 MiB of HBM per device.

```python
import jax
import jax.numpy as jnp
from jax import lax

DIN = 64
DOUT = 64
TROWS = 512
QBLK = 16
QB_DEV = 4
F = 4096
LAYERS = 16
SLOTS = 24
TRAIN = 16384
QUERIES = 2048
N_EX = 32


def factor_draw(key, width):
    noise = jax.random.normal(jax.random.fold_in(key, 1), (LAYERS, width, width), jnp.float32)
    mirror = (noise + jnp.swapaxes(noise, 1, 2)) / jnp.sqrt(2.0 * width)
    scales = jnp.exp(jax.random.uniform(jax.random.fold_in(key, 2), (LAYERS, 1, 1), jnp.float32, -0.7, 0.7))
    return scales * (jnp.eye(width, dtype=jnp.float32)[None] + 0.35 * mirror)


def draw_in_precond(key, part):
    return factor_draw(jax.random.fold_in(key, 11), DIN)


def draw_out_precond(key, part):
    return factor_draw(jax.random.fold_in(key, 12), DOUT)


def draw_pair_blocks(key, part):
    owner_keys = jax.random.split(jax.random.fold_in(key, 7), N_EX)
    sources = jax.vmap(lambda subkey: jax.random.permutation(subkey, N_EX))(owner_keys)[:, :SLOTS]
    within = jax.random.randint(jax.random.fold_in(key, 8), (N_EX, SLOTS), 0, QB_DEV)
    filled = jax.random.randint(jax.random.fold_in(key, 9), (N_EX,), SLOTS // 4, SLOTS + 1)
    full_owner = jax.random.randint(jax.random.fold_in(key, 10), (), 0, N_EX)
    filled = jnp.where(jnp.arange(N_EX) == full_owner, SLOTS, filled)
    block_ids = sources * QB_DEV + within
    block_ids = jnp.where(jnp.arange(SLOTS)[None, :] < filled[:, None], block_ids, -1)
    return block_ids.reshape(-1).astype(jnp.int32)


def block_scale(rng, extent, cuts, smallest, largest):
    factor_of = 1.0
    for position, blocks in cuts:
        draws = jax.random.uniform(jax.random.fold_in(jax.random.fold_in(rng, 6), position), (blocks,), jnp.float32, smallest / len(cuts), largest / len(cuts))
        factor_of = factor_of * jnp.repeat(jnp.exp(draws), extent[position] // blocks).reshape((-1,) + (1,) * (len(extent) - 1 - position))
    return factor_of


def normal_values(rng, dims, scale, bound, pieces=(), kind=jnp.bfloat16):
    array = jax.random.normal(rng, dims, jnp.float32) * scale
    if len(pieces) > 0:
        array = block_scale(rng, dims, pieces, -0.22, 0.18) * array
    return jnp.clip(array, min=-bound, max=bound).astype(kind)


def setup_inputs(seed: int = 0) -> dict:
    seeds = jax.random.split(jax.random.key(seed), 6)
    train_grads = normal_values(seeds[0], (TRAIN, LAYERS, F), 0.0625, 0.3984375, ((0, 32), (1, 16)))
    query_grads = normal_values(seeds[1], (QUERIES, LAYERS, F), 0.0625, 0.3984375, ((0, 32), (1, 16)))
    in_precond = draw_in_precond(jax.random.fold_in(seeds[5], 71), 0)
    out_precond = draw_out_precond(jax.random.fold_in(seeds[5], 71), 0)
    pair_blocks = draw_pair_blocks(jax.random.fold_in(seeds[5], 71), 0)
    return dict(train_grads=train_grads, query_grads=query_grads, in_precond=in_precond, out_precond=out_precond, pair_blocks=pair_blocks)


def precondition(queries, in_precond, out_precond):
    matrices = queries.astype(jnp.float32).reshape(queries.shape[0], LAYERS, DOUT, DIN)
    left_side = jnp.einsum("loj,rlji->rloi", out_precond, matrices, precision=lax.Precision.HIGHEST)
    precond = jnp.einsum("rloi,lik->rlok", left_side, in_precond, precision=lax.Precision.HIGHEST)
    return precond.reshape(queries.shape[0], LAYERS * F).astype(jnp.bfloat16)


def reference(train_grads, query_grads, in_precond, out_precond, pair_blocks):
    prepared = precondition(query_grads, in_precond, out_precond)
    train_flat = train_grads.reshape(TRAIN, LAYERS * F)

    def one_pair(pair_index):
        block_id = pair_blocks[pair_index]
        owner_id = (pair_index // SLOTS).astype(jnp.int32)
        query_start = (jnp.maximum(block_id, 0) * QBLK).astype(jnp.int32)
        query_rows = lax.dynamic_slice_in_dim(prepared, query_start, QBLK, 0)
        train_rows = lax.dynamic_slice_in_dim(train_flat, (owner_id * TROWS).astype(jnp.int32), TROWS, 0)
        tile_value = jnp.dot(query_rows, train_rows.T, preferred_element_type=jnp.float32)
        return jnp.where(block_id >= 0, tile_value, jnp.zeros_like(tile_value))

    tiles = lax.map(one_pair, jnp.arange(N_EX * SLOTS, dtype=jnp.int32))
    return jnp.transpose(tiles, (1, 0, 2))
```

```python
import functools

import jax
import jax.numpy as jnp
from jax import lax
from jax.experimental import pallas as pl
from jax.experimental.pallas import tpu as pltpu
from jax.sharding import PartitionSpec as P

MESH = pl.DeviceIdType.MESH
NX = 4
HELD = 4
NC = 4
LANES = 128
LAG = 3


def precondition(blocks, in_precond, out_precond):
    matrices = blocks.astype(jnp.float32).reshape((-1, out_precond.shape[-1], in_precond.shape[-1]))
    left_side = jnp.einsum("oj,rji->roi", out_precond, matrices, precision=lax.Precision.HIGHEST)
    precond = jnp.einsum("roi,ik->rok", left_side, in_precond, precision=lax.Precision.HIGHEST)
    return precond.reshape(matrices.shape[0], -1).astype(jnp.bfloat16)


def kernel(
    n_ex, layers, slots,
    pick_ref, pair_ref, own_hbm, train_hbm, out_ref,
    ag, recv, stage, fwd, train_v, acc, send_pair, recv_pair, send_one, recv_one, total,
    load_sem, ag_send, ag_recv, x_send, x_recv, fwd_send, fwd_recv, pair_send, one_send, pair_recv, one_recv,
):
    ny = n_ex // NX
    half = ny // 2
    cuts = acc.shape[0]
    rows = layers
    regular = NC * (half - 1)
    items = regular + NC // 2
    last = ny - 1
    ex = lax.axis_index("ex")
    lay = lax.axis_index("layer")
    y, x = ex // NX, ex % NX
    up = ((y + 1) % ny) * NX + x
    down = ((y + ny - 1) % ny) * NX + x
    right = y * NX + (x + 1) % NX
    left = y * NX + (x + NX - 1) % NX
    across = y * NX + (x + 2) % NX

    def load_own():
        return pltpu.make_async_copy(own_hbm, ag.at[pl.ds(0, NC)], load_sem.at[NC])

    def load_train(c):
        width = train_v.shape[2]
        return pltpu.make_async_copy(train_hbm.at[:, pl.ds(c * width, width)], train_v.at[c], load_sem.at[c])

    load_own().start()
    for c in range(NC):
        load_train(c).start()

    barrier = pltpu.get_barrier_semaphore()
    for peer in (up, down, right, left):
        pl.semaphore_signal(barrier, inc=1, device_id={"ex": peer}, device_id_type=MESH)

    @pl.loop(1, layers)
    def _(r):
        pl.semaphore_signal(barrier, inc=1, device_id={"layer": (lay + r) % layers}, device_id_type=MESH)

    acc[...] = jnp.zeros_like(acc)
    load_own().wait()
    pl.semaphore_wait(barrier, 4 + layers - 1)

    def send_along(src, dst, sem, peer):
        pltpu.make_async_remote_copy(
            src_ref=ag.at[src], dst_ref=ag.at[dst], send_sem=ag_send, recv_sem=ag_recv.at[sem],
            device_id={"ex": peer}, device_id_type=MESH,
        ).start()

    def plus(src, m):
        send_along(src, NC + m, m, up)

    def minus(src, m):
        send_along(src, NC + items + m, items + m, down)

    def wait_along(m):
        for side in range(2):
            there = ag.at[NC + side * items + m]
            pltpu.make_async_copy(there, there, ag_recv.at[side * items + m]).wait()

    for c in range(NC):
        plus(c, c)
        minus(c, c)

    def choose(src, label, c, row):
        blocks = [ag[src, pl.ds(b * rows, rows), :] for b in range(HELD)]
        for j, to in enumerate((ex, right, left, across)):
            want = pick_ref[to * n_ex + row * NX + x]
            v = blocks[HELD - 1]
            for b in range(HELD - 1):
                v = jnp.where(want == b, blocks[b], v)
            if j == 0:
                recv[c, label, pl.ds(0, rows), :] = v
            else:
                stage[c, label, j - 1] = v

    def push(label, c, via):
        def one(j, dst, sem, peer):
            pltpu.make_async_remote_copy(
                src_ref=stage.at[c, label, j], dst_ref=dst, send_sem=x_send, recv_sem=sem,
                device_id={"ex": peer}, device_id_type=MESH,
            ).start()

        one(2, fwd.at[c, label], fwd_recv.at[c, label], via)
        one(0, recv.at[c, label, pl.ds(rows, rows)], x_recv.at[c, label], right)
        one(1, recv.at[c, label, pl.ds(2 * rows, rows)], x_recv.at[c, label], left)

    def relay(label, c, via):
        here = fwd.at[c, label]
        pltpu.make_async_copy(here, here, fwd_recv.at[c, label]).wait()
        pltpu.make_async_remote_copy(
            src_ref=here, dst_ref=recv.at[c, label, pl.ds(3 * rows, rows)], send_sem=fwd_send,
            recv_sem=x_recv.at[c, label], device_id={"ex": via}, device_id_type=MESH,
        ).start()

    def arrived(label, c):
        there = recv.at[c, label, pl.ds(rows, 3 * rows)]
        pltpu.make_async_copy(there, there, x_recv.at[c, label]).wait()

    def multiply(label, c, count):
        for i in range(count):
            arrived(label + i, c)
        tall = count * NX * rows
        block = recv[c, pl.ds(label, count)].reshape(tall, recv.shape[3])
        where = pl.ds(pl.multiple_of(label * NX * rows, NX * rows), tall)
        product = lax.dot_general(
            block, train_v[c], (((1,), (1,)), ((), ())), preferred_element_type=jnp.float32
        )
        for n in range(cuts):
            acc[n, where, :] += product[:, n * LANES : (n + 1) * LANES]

    def scatter(src, dst, out_sem, sem):
        @pl.loop(1, layers)
        def _(r):
            to = (lay + r) % layers
            pltpu.make_async_remote_copy(
                src_ref=src.at[to], dst_ref=dst.at[r - 1], send_sem=out_sem, recv_sem=sem,
                device_id={"layer": to}, device_id_type=MESH,
            ).start()

    def reduce_pair(g):
        base = (2 * g + 1) * NX * rows

        for a in range(rows):
            for n in range(cuts):
                v = acc[n, pl.ds(base + a, 2 * NX, stride=rows), :]
                send_pair[g, a, pl.ds(n * 2 * NX, 2 * NX), :] = v
        scatter(send_pair.at[g], recv_pair.at[g], pair_send, pair_recv.at[g])

    def reduce_one(i):
        base = (0 if i == 0 else last) * NX * rows

        for a in range(rows):
            for n in range(cuts):
                v = acc[n, pl.ds(base + a, NX, stride=rows), :]
                send_one[i, a, pl.ds(n * NX, NX), :] = v
        scatter(send_one.at[i], recv_one.at[i], one_send, one_recv.at[i])

    def own_via(c):
        return right if c % 2 == 0 else left

    for c in range(NC):
        choose(c, 0, c, y)
    for c in range(NC):
        push(0, c, own_via(c))

    def labels(m):
        k = m // NC + 1
        return 2 * k - 1, 2 * k, m % NC

    def relay_step(m):
        a, b, c = labels(m)
        relay(a, c, right)
        relay(b, c, left)

    def multiply_step(m):
        a, _, c = labels(m)
        multiply(a, c, 2)

    @pl.loop(0, regular)
    def _(m):
        k = m // NC + 1
        a, b, c = labels(m)
        wait_along(m)

        @pl.when(m < items - NC)
        def _():
            plus(NC + m, m + NC)

        @pl.when((m < regular - NC) | (m >= regular - NC // 2))
        def _():
            minus(NC + items + m, jnp.where(m < regular - NC, m + NC, m + NC // 2))

        choose(NC + m, a, c, (y + ny - k) % ny)
        choose(NC + items + m, b, c, (y + k) % ny)
        push(a, c, right)
        push(b, c, left)

        @pl.when(m == 0)
        def _():
            for i in range(NC):
                relay(0, i, own_via(i))
                load_train(i).wait()

        @pl.when(m > 0)
        def _():
            relay_step(m - 1)

        @pl.when(m == 2)
        def _():
            @pl.loop(0, NC)
            def _(i):
                multiply(0, i, 1)

            reduce_one(0)

        @pl.when(m >= LAG)
        def _():
            multiply_step(m - LAG)

        for g in range(half - 1):
            if NC * g + NC - 1 + LAG < regular:

                @pl.when(m == NC * g + NC - 1 + LAG)
                def _():
                    reduce_pair(g)

    opposite = (y + half) % ny
    spots = [((t, right), (NC // 2 + t, left)) for t in range(NC // 2)]
    for t, spot in enumerate(spots):
        m = regular + t
        wait_along(m)
        for side, (c, _) in enumerate(spot):
            choose(NC + side * items + m, last, c, opposite)
        for c, via in spot:
            push(last, c, via)
        if t == 0:
            relay_step(regular - 1)
        else:
            for c, via in spots[t - 1]:
                relay(last, c, via)
        multiply_step(m - LAG)
    for c, via in spots[-1]:
        relay(last, c, via)
    for m in range(regular + len(spots) - LAG, regular):
        multiply_step(m)
    reduce_pair(half - 2)
    for spot in spots:
        for c, _ in spot:
            multiply(last, c, 1)
    reduce_one(1)

    def take_pair(g):
        there = recv_pair.at[g]
        pltpu.make_async_copy(there, there, pair_recv.at[g]).wait()
        v = send_pair[g, lay]
        for r in range(layers - 1):
            v = v + recv_pair[g, r]
        for n in range(cuts):
            where = pl.ds((2 * g + 1) * NX, 2 * NX)
            total[where, pl.ds(n * LANES, LANES)] = v[n * 2 * NX : (n + 1) * 2 * NX]

    def take_one(i):
        there = recv_one.at[i]
        pltpu.make_async_copy(there, there, one_recv.at[i]).wait()
        v = send_one[i, lay]
        for r in range(layers - 1):
            v = v + recv_one[i, r]
        for n in range(cuts):
            where = pl.ds((0 if i == 0 else last) * NX, NX)
            total[where, pl.ds(n * LANES, LANES)] = v[n * NX : (n + 1) * NX]

    take_one(0)
    for g in range(half - 1):
        take_pair(g)
    take_one(1)

    for p in range(slots):
        block = pair_ref[ex * slots + p]
        source = jnp.maximum(block, 0) // HELD
        dy = (source // NX - y + ny) % ny
        dx = (source % NX - x + NX) % NX
        label = jnp.where(dy == half, last, jnp.where(dy < half, 2 * dy, 2 * (ny - dy) - 1))
        off = jnp.where(dx == 3, 1, jnp.where(dx == 1, 2, jnp.where(dx == 2, 3, 0)))
        v = total[pl.ds(label * NX + off, 1), :]
        out_ref[0, pl.ds(p, 1), :] = jnp.where(block >= 0, v, jnp.zeros_like(v))

    sent = ag.at[pl.ds(NC, 2 * items)]
    pltpu.make_async_copy(sent, sent, ag_send).wait()
    pltpu.make_async_copy(stage, stage, x_send).wait()
    pltpu.make_async_copy(fwd, fwd, fwd_send).wait()
    pltpu.make_async_copy(recv_pair, recv_pair, pair_send).wait()
    pltpu.make_async_copy(recv_one, recv_one, one_send).wait()


def shards(train_grads, query_grads, in_precond, out_precond, pair_blocks):
    n_ex = lax.axis_size("ex")
    layers = lax.axis_size("layer")
    features = train_grads.shape[2]
    width = features // NC
    held_rows = query_grads.shape[0]
    rows = held_rows // HELD
    train_rows = train_grads.shape[0]
    cuts = train_rows // LANES
    slots = pair_blocks.shape[0] // n_ex
    ny = n_ex // NX
    half = ny // 2
    items = NC * (half - 1) + NC // 2

    wanted = pair_blocks.reshape(n_ex, slots)
    hit = (wanted[:, :, None] // HELD == jnp.arange(n_ex)[None, None, :]) & (wanted[:, :, None] >= 0)
    pick = jnp.sum(jnp.where(hit, wanted[:, :, None] % HELD, 0), axis=1).astype(jnp.int32).reshape(-1)

    own = precondition(query_grads[:, 0, :], in_precond[0], out_precond[0])
    own = own.reshape(held_rows, NC, width).transpose(1, 0, 2)
    train = train_grads.reshape(train_rows, features)

    bf16, f32 = jnp.bfloat16, jnp.float32
    dma = pltpu.SemaphoreType.DMA
    return pl.pallas_call(
        functools.partial(kernel, n_ex, layers, slots),
        out_shape=jax.ShapeDtypeStruct((1, slots, train_rows), f32),
        in_specs=[
            pl.BlockSpec(memory_space=pltpu.SMEM),
            pl.BlockSpec(memory_space=pltpu.SMEM),
            pl.BlockSpec(memory_space=pl.ANY),
            pl.BlockSpec(memory_space=pl.ANY),
        ],
        out_specs=pl.BlockSpec(memory_space=pltpu.VMEM),
        scratch_shapes=[
            pltpu.VMEM((NC + 2 * items, held_rows, width), bf16),
            pltpu.VMEM((NC, ny, NX * rows, width), bf16),
            pltpu.VMEM((NC, ny, 3, rows, width), bf16),
            pltpu.VMEM((NC, ny, rows, width), bf16),
            pltpu.VMEM((NC, train_rows, width), bf16),
            pltpu.VMEM((cuts, ny * NX * rows, LANES), f32),
            pltpu.VMEM((half - 1, layers, cuts * 2 * NX, LANES), f32),
            pltpu.VMEM((half - 1, layers - 1, cuts * 2 * NX, LANES), f32),
            pltpu.VMEM((2, layers, cuts * NX, LANES), f32),
            pltpu.VMEM((2, layers - 1, cuts * NX, LANES), f32),
            pltpu.VMEM((ny * NX, train_rows), f32),
            dma((NC + 1,)),
            dma,
            dma((2 * items,)),
            dma,
            dma((NC, ny)),
            dma,
            dma((NC, ny)),
            dma,
            dma,
            dma((half - 1,)),
            dma((2,)),
        ],
        compiler_params=pltpu.CompilerParams(
            collective_id=0, has_side_effects=True, vmem_limit_bytes=48 * 1024 * 1024
        ),
        name="tiles",
    )(pick, pair_blocks, own, train)


def solution(mesh):
    in_specs = (
        P("ex", "layer", None),
        P("ex", "layer", None),
        P("layer", None, None),
        P("layer", None, None),
        P(),
    )
    out_specs = P("layer", "ex", None)
    return jax.shard_map(shards, mesh=mesh, in_specs=in_specs, out_specs=out_specs, check_vma=False)
```

```python
import functools

import jax
import jax.numpy as jnp
from jax import lax
from jax.experimental import pallas as pl
from jax.experimental.pallas import tpu as pltpu
from jax.sharding import PartitionSpec as P

MESH = pl.DeviceIdType.MESH
NX = 4
HELD = 4
NC = 4
LANES = 128
LAG = 3


def wanted_words(pair_ref, destinations, slots, x):
    def step(p, words):
        out = []
        for word, to in zip(words, destinations):
            block = pair_ref[to * slots + p]
            source = jnp.right_shift(block, 2)
            row = jnp.right_shift(source, 2)
            mine = (block >= 0) & (jnp.bitwise_and(source, NX - 1) == x)
            bits = jnp.left_shift(jnp.bitwise_and(block, HELD - 1), 2 * jnp.bitwise_and(row, 15))
            out.append(word | jnp.where(mine, bits, 0))
        return tuple(out)

    return lax.fori_loop(0, slots, step, (jnp.int32(0),) * len(destinations))


def halves(v):
    high = v.astype(jnp.bfloat16)
    return high, (v - high.astype(jnp.float32)).astype(jnp.bfloat16)


def one_hot(condition):
    return jnp.where(condition, 1.0, 0.0).astype(jnp.bfloat16)


def exact(a, b):
    return jnp.dot(a, b, preferred_element_type=jnp.float32)


def spread_in(factor):
    n = factor.shape[0]
    down = lax.broadcasted_iota(jnp.int32, (2 * n, n), 0)
    across = lax.broadcasted_iota(jnp.int32, (2 * n, n), 1)
    below = one_hot(down % n == across)
    down = lax.broadcasted_iota(jnp.int32, (n, 2 * n), 0)
    across = lax.broadcasted_iota(jnp.int32, (n, 2 * n), 1)
    beside = one_hot(across % n == down)
    down = lax.broadcasted_iota(jnp.int32, (2 * n, 2 * n), 0)
    across = lax.broadcasted_iota(jnp.int32, (2 * n, 2 * n), 1)
    same = down // n == across // n
    out = []
    for half in halves(factor):
        full = exact(exact(below, half).astype(jnp.bfloat16), beside)
        out.append(jnp.where(same, full, 0.0).astype(jnp.bfloat16))
    return jnp.concatenate(out, axis=0)


def spread_out(factor):
    n = factor.shape[0]
    high, low = halves(factor)
    down = lax.broadcasted_iota(jnp.int32, (n, n), 0)
    across = lax.broadcasted_iota(jnp.int32, (n, n), 1)
    order = one_hot(across == 2 * (down % (n // 2)) + down // (n // 2))
    down = lax.broadcasted_iota(jnp.int32, (n, 3 * n), 0)
    across = lax.broadcasted_iota(jnp.int32, (n, 3 * n), 1)
    inner = across % n
    hit = down == 2 * (inner % (n // 2)) + inner // (n // 2)
    first = one_hot(hit & (across < 2 * n))
    second = one_hot(hit & (across >= 2 * n))
    high = exact(exact(order, high).astype(jnp.bfloat16), first)
    low = exact(exact(order, low).astype(jnp.bfloat16), second)
    return (high + low).astype(jnp.bfloat16)


def prepare(query_v, left_factor, right_factor, mid):
    held, features = query_v.shape
    pairs = features // LANES
    n = LANES // 2
    lane = lax.broadcasted_iota(jnp.int32, (pairs, LANES), 1)
    low = lane < n

    for d in range(pairs):
        g = query_v[:, d * LANES : (d + 1) * LANES]
        both = jnp.concatenate([g, g], axis=1)
        mid[pl.ds(d * held, held), :] = exact(both, right_factor)

    def side_by_side(t):
        u0 = mid[pl.ds(2 * t, pairs, stride=held), :]
        u1 = mid[pl.ds(2 * t + 1, pairs, stride=held), :]
        even = jnp.where(low, u0, pltpu.roll(u1, n, 1))
        odd = jnp.where(low, pltpu.roll(u0, n, 1), u1)
        return halves(jnp.concatenate([even, odd], axis=0))

    def apart(t, z):
        even, odd = z[:pairs], z[pairs:]
        mid[pl.ds(2 * t, pairs, stride=held), :] = jnp.where(low, even, pltpu.roll(odd, n, 1))
        mid[pl.ds(2 * t + 1, pairs, stride=held), :] = jnp.where(low, pltpu.roll(even, n, 1), odd)

    for t in range(0, held // 2, 2):
        (h0, l0), (h1, l1) = side_by_side(t), side_by_side(t + 1)
        high = jnp.concatenate([h0, h1], axis=1)
        rest = jnp.concatenate([l0, l1], axis=1)
        z = exact(left_factor, jnp.concatenate([high, rest, high], axis=0))
        apart(t, z[:, :LANES])
        apart(t + 1, z[:, LANES:])


def finish(mid, own):
    chunks, held, width = own.shape
    each = width // LANES
    for d in range(chunks * each):
        own[d // each, :, pl.ds(d % each * LANES, LANES)] = mid[pl.ds(d * held, held), :].astype(jnp.bfloat16)


def prepare_kernel(n_ex, slots, pair_ref, query_ref, in_ref, out_pre_ref, own_ref, words_ref, mid):
    ex = lax.axis_index("ex")
    y, x = ex // NX, ex % NX
    to = [y * NX + (x + d) % NX for d in (0, 1, 3, 2)]
    for j, word in enumerate(wanted_words(pair_ref, to, slots, x)):
        words_ref[j] = word
    prepare(query_ref, spread_out(out_pre_ref[0]), spread_in(in_ref[0]), mid)
    finish(mid, own_ref)


def kernel(
    n_ex, layers, slots,
    words_ref, pair_ref, own_hbm, train_hbm, out_ref,
    own, ag, recv, stage, fwd, train_v, acc, send_pair, recv_pair, send_one, recv_one, total,
    load_sem, ag_send, ag_recv, x_send, x_recv, fwd_send, fwd_recv, pair_send, one_send, pair_recv, one_recv,
):
    ny = n_ex // NX
    half = ny // 2
    cuts = acc.shape[0]
    rows = layers
    regular = NC * (half - 1)
    items = regular + NC // 2
    last = ny - 1
    ex = lax.axis_index("ex")
    lay = lax.axis_index("layer")
    y, x = ex // NX, ex % NX
    up = ((y + 1) % ny) * NX + x
    down = ((y + ny - 1) % ny) * NX + x
    right = y * NX + (x + 1) % NX
    left = y * NX + (x + NX - 1) % NX
    across = y * NX + (x + 2) % NX

    def load_own():
        return pltpu.make_async_copy(own_hbm, own, load_sem.at[NC])

    def load_train(c):
        width = train_v.shape[2]
        return pltpu.make_async_copy(train_hbm.at[:, pl.ds(c * width, width)], train_v.at[c], load_sem.at[c])

    load_own().start()
    for c in range(NC):
        load_train(c).start()

    barrier = pltpu.get_barrier_semaphore()
    for peer in (up, down, right, left):
        pl.semaphore_signal(barrier, inc=1, device_id={"ex": peer}, device_id_type=MESH)

    @pl.loop(1, layers)
    def _(r):
        pl.semaphore_signal(barrier, inc=1, device_id={"layer": (lay + r) % layers}, device_id_type=MESH)

    acc[...] = jnp.zeros_like(acc)
    load_own().wait()
    pl.semaphore_wait(barrier, 4 + layers - 1)
    words = [words_ref[j] for j in range(NX)]

    def send_along(src, dst, peer):
        pltpu.make_async_remote_copy(
            src_ref=src, dst_ref=ag.at[dst], send_sem=ag_send, recv_sem=ag_recv.at[dst],
            device_id={"ex": peer}, device_id_type=MESH,
        ).start()

    def plus(src, m):
        send_along(src, m, up)

    def minus(src, m):
        send_along(src, items + m, down)

    def wait_along(m):
        for side in range(2):
            there = ag.at[side * items + m]
            pltpu.make_async_copy(there, there, ag_recv.at[side * items + m]).wait()

    for c in range(NC):
        plus(own.at[c], c)
        minus(own.at[c], c)

    def choose(src, label, c, row):
        blocks = [src[pl.ds(b * rows, rows), :] for b in range(HELD)]
        for j, word in enumerate(words):
            want = jnp.bitwise_and(jnp.right_shift(word, 2 * row), HELD - 1)
            v = blocks[HELD - 1]
            for b in range(HELD - 1):
                v = jnp.where(want == b, blocks[b], v)
            if j == 0:
                recv[c, label, pl.ds(0, rows), :] = v
            else:
                stage[c, label, j - 1] = v

    def push(label, c, via):
        def one(j, dst, sem, peer):
            pltpu.make_async_remote_copy(
                src_ref=stage.at[c, label, j], dst_ref=dst, send_sem=x_send, recv_sem=sem,
                device_id={"ex": peer}, device_id_type=MESH,
            ).start()

        one(2, fwd.at[c, label], fwd_recv.at[c, label], via)
        one(0, recv.at[c, label, pl.ds(rows, rows)], x_recv.at[c, label], right)
        one(1, recv.at[c, label, pl.ds(2 * rows, rows)], x_recv.at[c, label], left)

    def relay(label, c, via):
        here = fwd.at[c, label]
        pltpu.make_async_copy(here, here, fwd_recv.at[c, label]).wait()
        pltpu.make_async_remote_copy(
            src_ref=here, dst_ref=recv.at[c, label, pl.ds(3 * rows, rows)], send_sem=fwd_send,
            recv_sem=x_recv.at[c, label], device_id={"ex": via}, device_id_type=MESH,
        ).start()

    def arrived(label, c):
        there = recv.at[c, label, pl.ds(rows, 3 * rows)]
        pltpu.make_async_copy(there, there, x_recv.at[c, label]).wait()

    def multiply(label, c, count):
        for i in range(count):
            arrived(label + i, c)
        tall = count * NX * rows
        block = recv[c, pl.ds(label, count)].reshape(tall, recv.shape[3])
        where = pl.ds(pl.multiple_of(label * NX * rows, NX * rows), tall)
        product = lax.dot_general(
            block, train_v[c], (((1,), (1,)), ((), ())), preferred_element_type=jnp.float32
        )
        for n in range(cuts):
            acc[n, where, :] += product[:, n * LANES : (n + 1) * LANES]

    def scatter(src, dst, out_sem, sem):
        @pl.loop(1, layers)
        def _(r):
            to = (lay + r) % layers
            pltpu.make_async_remote_copy(
                src_ref=src.at[to], dst_ref=dst.at[r - 1], send_sem=out_sem, recv_sem=sem,
                device_id={"layer": to}, device_id_type=MESH,
            ).start()

    def reduce_pair(g):
        base = (2 * g + 1) * NX * rows

        for a in range(rows):
            for n in range(cuts):
                v = acc[n, pl.ds(base + a, 2 * NX, stride=rows), :]
                send_pair[g, a, pl.ds(n * 2 * NX, 2 * NX), :] = v
        scatter(send_pair.at[g], recv_pair.at[g], pair_send, pair_recv.at[g])

    def reduce_one(i):
        base = (0 if i == 0 else last) * NX * rows

        for a in range(rows):
            for n in range(cuts):
                v = acc[n, pl.ds(base + a, NX, stride=rows), :]
                send_one[i, a, pl.ds(n * NX, NX), :] = v
        scatter(send_one.at[i], recv_one.at[i], one_send, one_recv.at[i])

    def own_via(c):
        return right if c % 2 == 0 else left

    for c in range(NC):
        choose(own.at[c], 0, c, y)
    for c in range(NC):
        push(0, c, own_via(c))

    def labels(m):
        k = m // NC + 1
        return 2 * k - 1, 2 * k, m % NC

    def relay_step(m):
        a, b, c = labels(m)
        relay(a, c, right)
        relay(b, c, left)

    def multiply_step(m):
        a, _, c = labels(m)
        multiply(a, c, 2)

    @pl.loop(0, regular)
    def _(m):
        k = m // NC + 1
        a, b, c = labels(m)
        wait_along(m)

        @pl.when(m < items - NC)
        def _():
            plus(ag.at[m], m + NC)

        @pl.when((m < regular - NC) | (m >= regular - NC // 2))
        def _():
            minus(ag.at[items + m], jnp.where(m < regular - NC, m + NC, m + NC // 2))

        choose(ag.at[m], a, c, (y + ny - k) % ny)
        choose(ag.at[items + m], b, c, (y + k) % ny)
        push(a, c, right)
        push(b, c, left)

        @pl.when(m == 0)
        def _():
            for i in range(NC):
                relay(0, i, own_via(i))
                load_train(i).wait()

        @pl.when(m > 0)
        def _():
            relay_step(m - 1)

        @pl.when(m == 2)
        def _():
            @pl.loop(0, NC)
            def _(i):
                multiply(0, i, 1)

            reduce_one(0)

        @pl.when(m >= LAG)
        def _():
            multiply_step(m - LAG)

        for g in range(half - 1):
            if NC * g + NC - 1 + LAG < regular:

                @pl.when(m == NC * g + NC - 1 + LAG)
                def _():
                    reduce_pair(g)

    opposite = (y + half) % ny
    spots = [((t, right), (NC // 2 + t, left)) for t in range(NC // 2)]
    for t, spot in enumerate(spots):
        m = regular + t
        wait_along(m)
        for side, (c, _) in enumerate(spot):
            choose(ag.at[side * items + m], last, c, opposite)
        for c, via in spot:
            push(last, c, via)
        if t == 0:
            relay_step(regular - 1)
        else:
            for c, via in spots[t - 1]:
                relay(last, c, via)
        if t < len(spots) - 1:
            multiply_step(m - LAG)
    for m in range(regular + len(spots) - 1 - LAG, regular):
        multiply_step(m)
    reduce_pair(half - 2)
    for c, via in spots[-1]:
        relay(last, c, via)
    for spot in spots:
        for c, _ in spot:
            multiply(last, c, 1)
    reduce_one(1)

    def take_pair(g):
        there = recv_pair.at[g]
        pltpu.make_async_copy(there, there, pair_recv.at[g]).wait()
        v = send_pair[g, lay]
        for r in range(layers - 1):
            v = v + recv_pair[g, r]
        for n in range(cuts):
            where = pl.ds((2 * g + 1) * NX, 2 * NX)
            total[where, pl.ds(n * LANES, LANES)] = v[n * 2 * NX : (n + 1) * 2 * NX]

    def take_one(i):
        there = recv_one.at[i]
        pltpu.make_async_copy(there, there, one_recv.at[i]).wait()
        v = send_one[i, lay]
        for r in range(layers - 1):
            v = v + recv_one[i, r]
        for n in range(cuts):
            where = pl.ds((0 if i == 0 else last) * NX, NX)
            total[where, pl.ds(n * LANES, LANES)] = v[n * NX : (n + 1) * NX]

    take_one(0)
    for g in range(half - 1):
        take_pair(g)
    take_one(1)

    for p in range(slots):
        block = pair_ref[ex * slots + p]
        source = jnp.maximum(block, 0) // HELD
        dy = (source // NX - y + ny) % ny
        dx = (source % NX - x + NX) % NX
        label = jnp.where(dy == half, last, jnp.where(dy < half, 2 * dy, 2 * (ny - dy) - 1))
        off = jnp.where(dx == 3, 1, jnp.where(dx == 1, 2, jnp.where(dx == 2, 3, 0)))
        v = total[pl.ds(label * NX + off, 1), :]
        out_ref[0, pl.ds(p, 1), :] = jnp.where(block >= 0, v, jnp.zeros_like(v))

    pltpu.make_async_copy(ag, ag, ag_send).wait()
    pltpu.make_async_copy(stage, stage, x_send).wait()
    pltpu.make_async_copy(fwd, fwd, fwd_send).wait()
    pltpu.make_async_copy(recv_pair, recv_pair, pair_send).wait()
    pltpu.make_async_copy(recv_one, recv_one, one_send).wait()


def shards(train_grads, query_grads, in_precond, out_precond, pair_blocks):
    n_ex = lax.axis_size("ex")
    layers = lax.axis_size("layer")
    features = train_grads.shape[2]
    width = features // NC
    held_rows = query_grads.shape[0]
    rows = held_rows // HELD
    train_rows = train_grads.shape[0]
    cuts = train_rows // LANES
    slots = pair_blocks.shape[0] // n_ex
    ny = n_ex // NX
    half = ny // 2
    items = NC * (half - 1) + NC // 2

    query = query_grads.reshape(held_rows, features)
    train = train_grads.reshape(train_rows, features)

    bf16, f32 = jnp.bfloat16, jnp.float32
    dma = pltpu.SemaphoreType.DMA
    whole = 67043328
    own, words = pl.pallas_call(
        functools.partial(prepare_kernel, n_ex, slots),
        out_shape=(
            jax.ShapeDtypeStruct((NC, held_rows, width), bf16),
            jax.ShapeDtypeStruct((NX,), jnp.int32),
        ),
        in_specs=[
            pl.BlockSpec(memory_space=pltpu.SMEM),
            pl.BlockSpec(memory_space=pltpu.VMEM),
            pl.BlockSpec(memory_space=pltpu.VMEM),
            pl.BlockSpec(memory_space=pltpu.VMEM),
        ],
        out_specs=(pl.BlockSpec(memory_space=pltpu.VMEM), pl.BlockSpec(memory_space=pltpu.SMEM)),
        scratch_shapes=[pltpu.VMEM((held_rows * features // LANES, LANES), f32)],
        compiler_params=pltpu.CompilerParams(vmem_limit_bytes=whole),
        name="prepare",
    )(pair_blocks, query, in_precond, out_precond)
    return pl.pallas_call(
        functools.partial(kernel, n_ex, layers, slots),
        out_shape=jax.ShapeDtypeStruct((1, slots, train_rows), f32),
        in_specs=[
            pl.BlockSpec(memory_space=pltpu.SMEM),
            pl.BlockSpec(memory_space=pltpu.SMEM),
            pl.BlockSpec(memory_space=pl.ANY),
            pl.BlockSpec(memory_space=pl.ANY),
        ],
        out_specs=pl.BlockSpec(memory_space=pltpu.VMEM),
        scratch_shapes=[
            pltpu.VMEM((NC, held_rows, width), bf16),
            pltpu.VMEM((2 * items, held_rows, width), bf16),
            pltpu.VMEM((NC, ny, NX * rows, width), bf16),
            pltpu.VMEM((NC, ny, 3, rows, width), bf16),
            pltpu.VMEM((NC, ny, rows, width), bf16),
            pltpu.VMEM((NC, train_rows, width), bf16),
            pltpu.VMEM((cuts, ny * NX * rows, LANES), f32),
            pltpu.VMEM((half - 1, layers, cuts * 2 * NX, LANES), f32),
            pltpu.VMEM((half - 1, layers - 1, cuts * 2 * NX, LANES), f32),
            pltpu.VMEM((2, layers, cuts * NX, LANES), f32),
            pltpu.VMEM((2, layers - 1, cuts * NX, LANES), f32),
            pltpu.VMEM((ny * NX, train_rows), f32),
            dma((NC + 1,)),
            dma,
            dma((2 * items,)),
            dma,
            dma((NC, ny)),
            dma,
            dma((NC, ny)),
            dma,
            dma,
            dma((half - 1,)),
            dma((2,)),
        ],
        compiler_params=pltpu.CompilerParams(
            collective_id=0, has_side_effects=True, vmem_limit_bytes=whole
        ),
        name="tiles",
    )(words, pair_blocks, own, train)


def solution(mesh):
    in_specs = (
        P("ex", "layer", None),
        P("ex", "layer", None),
        P("layer", None, None),
        P("layer", None, None),
        P(),
    )
    out_specs = P("layer", "ex", None)
    return jax.shard_map(shards, mesh=mesh, in_specs=in_specs, out_specs=out_specs, check_vma=False)
```

```python
import functools

import jax
import jax.numpy as jnp
from jax import lax
from jax.experimental import pallas as pl
from jax.experimental.pallas import tpu as pltpu
from jax.sharding import PartitionSpec as P

MESH = pl.DeviceIdType.MESH
NX = 4
HELD = 4
NC = 4
LANES = 128
LAG = 3


def wanted_words(pair_ref, destinations, slots, x):
    def step(p, words):
        out = []
        for word, to in zip(words, destinations):
            block = pair_ref[to * slots + p]
            source = jnp.right_shift(block, 2)
            row = jnp.right_shift(source, 2)
            mine = (block >= 0) & (jnp.bitwise_and(source, NX - 1) == x)
            bits = jnp.left_shift(jnp.bitwise_and(block, HELD - 1), 2 * jnp.bitwise_and(row, 15))
            out.append(word | jnp.where(mine, bits, 0))
        return tuple(out)

    return lax.fori_loop(0, slots, step, (jnp.int32(0),) * len(destinations))


def halves(v):
    high = v.astype(jnp.bfloat16)
    return high, (v - high.astype(jnp.float32)).astype(jnp.bfloat16)


def one_hot(condition):
    return jnp.where(condition, 1.0, 0.0).astype(jnp.bfloat16)


def exact(a, b):
    return jnp.dot(a, b, preferred_element_type=jnp.float32)


def spread_in(factor):
    n = factor.shape[0]
    down = lax.broadcasted_iota(jnp.int32, (2 * n, n), 0)
    across = lax.broadcasted_iota(jnp.int32, (2 * n, n), 1)
    below = one_hot(down % n == across)
    down = lax.broadcasted_iota(jnp.int32, (n, 2 * n), 0)
    across = lax.broadcasted_iota(jnp.int32, (n, 2 * n), 1)
    beside = one_hot(across % n == down)
    down = lax.broadcasted_iota(jnp.int32, (2 * n, 2 * n), 0)
    across = lax.broadcasted_iota(jnp.int32, (2 * n, 2 * n), 1)
    same = down // n == across // n
    out = []
    for half in halves(factor):
        full = exact(exact(below, half).astype(jnp.bfloat16), beside)
        out.append(jnp.where(same, full, 0.0).astype(jnp.bfloat16))
    return jnp.concatenate(out, axis=0)


def spread_out(factor):
    n = factor.shape[0]
    high, low = halves(factor)
    down = lax.broadcasted_iota(jnp.int32, (n, n), 0)
    across = lax.broadcasted_iota(jnp.int32, (n, n), 1)
    order = one_hot(across == 2 * (down % (n // 2)) + down // (n // 2))
    down = lax.broadcasted_iota(jnp.int32, (n, 3 * n), 0)
    across = lax.broadcasted_iota(jnp.int32, (n, 3 * n), 1)
    inner = across % n
    hit = down == 2 * (inner % (n // 2)) + inner // (n // 2)
    first = one_hot(hit & (across < 2 * n))
    second = one_hot(hit & (across >= 2 * n))
    high = exact(exact(order, high).astype(jnp.bfloat16), first)
    low = exact(exact(order, low).astype(jnp.bfloat16), second)
    return (high + low).astype(jnp.bfloat16)


def prepare(query_v, left_factor, right_factor, mid, turned):
    held, features = query_v.shape
    pairs = features // LANES
    n = LANES // 2
    lane = lax.broadcasted_iota(jnp.int32, (pairs, LANES), 1)
    low = lane < n

    for d in range(pairs):
        g = query_v[:, d * LANES : (d + 1) * LANES]
        both = jnp.concatenate([g, g], axis=1)
        mid[pl.ds(d * held, held), :] = exact(both, right_factor)

    def side_by_side(t):
        u0 = mid[pl.ds(2 * t, pairs, stride=held), :]
        u1 = mid[pl.ds(2 * t + 1, pairs, stride=held), :]
        even = jnp.where(low, u0, pltpu.roll(u1, n, 1))
        odd = jnp.where(low, pltpu.roll(u0, n, 1), u1)
        return halves(jnp.concatenate([even, odd], axis=0))

    def apart(t, z):
        even, odd = z[:pairs], z[pairs:]
        turned[pl.ds(2 * t * pairs, pairs), :] = jnp.where(low, even, pltpu.roll(odd, n, 1))
        turned[pl.ds((2 * t + 1) * pairs, pairs), :] = jnp.where(low, pltpu.roll(even, n, 1), odd)

    for t in range(0, held // 2, 2):
        (h0, l0), (h1, l1) = side_by_side(t), side_by_side(t + 1)
        high = jnp.concatenate([h0, h1], axis=1)
        rest = jnp.concatenate([l0, l1], axis=1)
        z = exact(left_factor, jnp.concatenate([high, rest, high], axis=0))
        apart(t, z[:, :LANES])
        apart(t + 1, z[:, LANES:])


def finish(turned, own):
    chunks, held, width = own.shape
    each = width // LANES
    pairs = chunks * each
    for d in range(pairs):
        v = turned[pl.ds(d, held, stride=pairs), :]
        own[d // each, :, pl.ds(d % each * LANES, LANES)] = v.astype(jnp.bfloat16)


def words_kernel(slots, pair_ref, words_ref):
    ex = lax.axis_index("ex")
    y, x = ex // NX, ex % NX
    to = [y * NX + (x + d) % NX for d in (0, 1, 3, 2)]
    for j, word in enumerate(wanted_words(pair_ref, to, slots, x)):
        words_ref[j] = word


def kernel(
    n_ex, layers, slots,
    words_ref, pair_ref, query_ref, in_ref, out_pre_ref, train_hbm, out_ref,
    mid, turned, made, own, ag, recv, stage, fwd, train_v, acc, send_pair, recv_pair, send_one, recv_one, total,
    load_sem, ag_send, ag_recv, x_send, x_recv, fwd_send, fwd_recv, pair_send, one_send, pair_recv, one_recv,
):
    ny = n_ex // NX
    half = ny // 2
    cuts = acc.shape[0]
    rows = layers
    regular = NC * (half - 1)
    items = regular + NC // 2
    last = ny - 1
    ex = lax.axis_index("ex")
    lay = lax.axis_index("layer")
    y, x = ex // NX, ex % NX
    up = ((y + 1) % ny) * NX + x
    down = ((y + ny - 1) % ny) * NX + x
    right = y * NX + (x + 1) % NX
    left = y * NX + (x + NX - 1) % NX
    across = y * NX + (x + 2) % NX

    def load_own():
        return pltpu.make_async_copy(made, own, load_sem.at[NC])

    def load_train(c):
        width = train_v.shape[2]
        return pltpu.make_async_copy(train_hbm.at[:, pl.ds(c * width, width)], train_v.at[c], load_sem.at[c])

    for c in range(NC):
        load_train(c).start()

    barrier = pltpu.get_barrier_semaphore()
    for peer in (up, down, right, left):
        pl.semaphore_signal(barrier, inc=1, device_id={"ex": peer}, device_id_type=MESH)

    @pl.loop(1, layers)
    def _(r):
        pl.semaphore_signal(barrier, inc=1, device_id={"layer": (lay + r) % layers}, device_id_type=MESH)

    acc[...] = jnp.zeros_like(acc)
    prepare(query_ref, spread_out(out_pre_ref[0]), spread_in(in_ref[0]), mid, turned)
    finish(turned, made)
    load_own().start()
    load_own().wait()
    pl.semaphore_wait(barrier, 4 + layers - 1)
    words = [words_ref[j] for j in range(NX)]

    def send_along(src, dst, peer):
        pltpu.make_async_remote_copy(
            src_ref=src, dst_ref=ag.at[dst], send_sem=ag_send, recv_sem=ag_recv.at[dst],
            device_id={"ex": peer}, device_id_type=MESH,
        ).start()

    def plus(src, m):
        send_along(src, m, up)

    def minus(src, m):
        send_along(src, items + m, down)

    def wait_along(m):
        for side in range(2):
            there = ag.at[side * items + m]
            pltpu.make_async_copy(there, there, ag_recv.at[side * items + m]).wait()

    for c in range(NC):
        plus(own.at[c], c)
        minus(own.at[c], c)

    def choose(src, label, c, row):
        blocks = [src[pl.ds(b * rows, rows), :] for b in range(HELD)]
        for j, word in enumerate(words):
            want = jnp.bitwise_and(jnp.right_shift(word, 2 * row), HELD - 1)
            v = blocks[HELD - 1]
            for b in range(HELD - 1):
                v = jnp.where(want == b, blocks[b], v)
            if j == 0:
                recv[c, label, pl.ds(0, rows), :] = v
            else:
                stage[c, label, j - 1] = v

    def push(label, c, via):
        def one(j, dst, sem, peer):
            pltpu.make_async_remote_copy(
                src_ref=stage.at[c, label, j], dst_ref=dst, send_sem=x_send, recv_sem=sem,
                device_id={"ex": peer}, device_id_type=MESH,
            ).start()

        one(2, fwd.at[c, label], fwd_recv.at[c, label], via)
        one(0, recv.at[c, label, pl.ds(rows, rows)], x_recv.at[c, label], right)
        one(1, recv.at[c, label, pl.ds(2 * rows, rows)], x_recv.at[c, label], left)

    def relay(label, c, via):
        here = fwd.at[c, label]
        pltpu.make_async_copy(here, here, fwd_recv.at[c, label]).wait()
        pltpu.make_async_remote_copy(
            src_ref=here, dst_ref=recv.at[c, label, pl.ds(3 * rows, rows)], send_sem=fwd_send,
            recv_sem=x_recv.at[c, label], device_id={"ex": via}, device_id_type=MESH,
        ).start()

    def arrived(label, c):
        there = recv.at[c, label, pl.ds(rows, 3 * rows)]
        pltpu.make_async_copy(there, there, x_recv.at[c, label]).wait()

    def multiply(label, c, count):
        for i in range(count):
            arrived(label + i, c)
        tall = count * NX * rows
        block = recv[c, pl.ds(label, count)].reshape(tall, recv.shape[3])
        where = pl.ds(pl.multiple_of(label * NX * rows, NX * rows), tall)
        product = lax.dot_general(
            block, train_v[c], (((1,), (1,)), ((), ())), preferred_element_type=jnp.float32
        )
        for n in range(cuts):
            acc[n, where, :] += product[:, n * LANES : (n + 1) * LANES]

    def scatter(src, dst, out_sem, sem):
        @pl.loop(1, layers)
        def _(r):
            to = (lay + r) % layers
            pltpu.make_async_remote_copy(
                src_ref=src.at[to], dst_ref=dst.at[r - 1], send_sem=out_sem, recv_sem=sem,
                device_id={"layer": to}, device_id_type=MESH,
            ).start()

    def reduce_pair(g):
        base = (2 * g + 1) * NX * rows

        for a in range(rows):
            for n in range(cuts):
                v = acc[n, pl.ds(base + a, 2 * NX, stride=rows), :]
                send_pair[g, a, pl.ds(n * 2 * NX, 2 * NX), :] = v
        scatter(send_pair.at[g], recv_pair.at[g], pair_send, pair_recv.at[g])

    def reduce_one(i):
        base = (0 if i == 0 else last) * NX * rows

        for a in range(rows):
            for n in range(cuts):
                v = acc[n, pl.ds(base + a, NX, stride=rows), :]
                send_one[i, a, pl.ds(n * NX, NX), :] = v
        scatter(send_one.at[i], recv_one.at[i], one_send, one_recv.at[i])

    def own_via(c):
        return right if c % 2 == 0 else left

    for c in range(NC):
        choose(own.at[c], 0, c, y)
    for c in range(NC):
        push(0, c, own_via(c))

    def labels(m):
        k = m // NC + 1
        return 2 * k - 1, 2 * k, m % NC

    def relay_step(m):
        a, b, c = labels(m)
        relay(a, c, right)
        relay(b, c, left)

    def multiply_step(m):
        a, _, c = labels(m)
        multiply(a, c, 2)

    @pl.loop(0, regular)
    def _(m):
        k = m // NC + 1
        a, b, c = labels(m)
        wait_along(m)

        @pl.when(m < items - NC)
        def _():
            plus(ag.at[m], m + NC)

        @pl.when((m < regular - NC) | (m >= regular - NC // 2))
        def _():
            minus(ag.at[items + m], jnp.where(m < regular - NC, m + NC, m + NC // 2))

        choose(ag.at[m], a, c, (y + ny - k) % ny)
        choose(ag.at[items + m], b, c, (y + k) % ny)
        push(a, c, right)
        push(b, c, left)

        @pl.when(m == 0)
        def _():
            for i in range(NC):
                relay(0, i, own_via(i))
                load_train(i).wait()

        @pl.when(m > 0)
        def _():
            relay_step(m - 1)

        @pl.when(m == 2)
        def _():
            @pl.loop(0, NC)
            def _(i):
                multiply(0, i, 1)

            reduce_one(0)

        @pl.when(m >= LAG)
        def _():
            multiply_step(m - LAG)

        for g in range(half - 1):
            if NC * g + NC - 1 + LAG < regular:

                @pl.when(m == NC * g + NC - 1 + LAG)
                def _():
                    reduce_pair(g)

    opposite = (y + half) % ny
    spots = [((t, right), (NC // 2 + t, left)) for t in range(NC // 2)]
    for t, spot in enumerate(spots):
        m = regular + t
        wait_along(m)
        for side, (c, _) in enumerate(spot):
            choose(ag.at[side * items + m], last, c, opposite)
        for c, via in spot:
            push(last, c, via)
        if t == 0:
            relay_step(regular - 1)
        else:
            for c, via in spots[t - 1]:
                relay(last, c, via)
        if t < len(spots) - 1:
            multiply_step(m - LAG)
    for m in range(regular + len(spots) - 1 - LAG, regular):
        multiply_step(m)
    reduce_pair(half - 2)
    for c, via in spots[-1]:
        relay(last, c, via)
    for spot in spots:
        for c, _ in spot:
            multiply(last, c, 1)
    reduce_one(1)

    def take_pair(g):
        there = recv_pair.at[g]
        pltpu.make_async_copy(there, there, pair_recv.at[g]).wait()
        v = send_pair[g, lay]
        for r in range(layers - 1):
            v = v + recv_pair[g, r]
        for n in range(cuts):
            where = pl.ds((2 * g + 1) * NX, 2 * NX)
            total[where, pl.ds(n * LANES, LANES)] = v[n * 2 * NX : (n + 1) * 2 * NX]

    def take_one(i):
        there = recv_one.at[i]
        pltpu.make_async_copy(there, there, one_recv.at[i]).wait()
        v = send_one[i, lay]
        for r in range(layers - 1):
            v = v + recv_one[i, r]
        for n in range(cuts):
            where = pl.ds((0 if i == 0 else last) * NX, NX)
            total[where, pl.ds(n * LANES, LANES)] = v[n * NX : (n + 1) * NX]

    take_one(0)
    for g in range(half - 1):
        take_pair(g)
    take_one(1)

    for p in range(slots):
        block = pair_ref[ex * slots + p]
        source = jnp.maximum(block, 0) // HELD
        dy = (source // NX - y + ny) % ny
        dx = (source % NX - x + NX) % NX
        label = jnp.where(dy == half, last, jnp.where(dy < half, 2 * dy, 2 * (ny - dy) - 1))
        off = jnp.where(dx == 3, 1, jnp.where(dx == 1, 2, jnp.where(dx == 2, 3, 0)))
        v = total[pl.ds(label * NX + off, 1), :]
        out_ref[0, pl.ds(p, 1), :] = jnp.where(block >= 0, v, jnp.zeros_like(v))

    pltpu.make_async_copy(ag, ag, ag_send).wait()
    pltpu.make_async_copy(stage, stage, x_send).wait()
    pltpu.make_async_copy(fwd, fwd, fwd_send).wait()
    pltpu.make_async_copy(recv_pair, recv_pair, pair_send).wait()
    pltpu.make_async_copy(recv_one, recv_one, one_send).wait()


def shards(train_grads, query_grads, in_precond, out_precond, pair_blocks):
    n_ex = lax.axis_size("ex")
    layers = lax.axis_size("layer")
    features = train_grads.shape[2]
    width = features // NC
    held_rows = query_grads.shape[0]
    rows = held_rows // HELD
    train_rows = train_grads.shape[0]
    cuts = train_rows // LANES
    slots = pair_blocks.shape[0] // n_ex
    ny = n_ex // NX
    half = ny // 2
    items = NC * (half - 1) + NC // 2

    query = query_grads.reshape(held_rows, features)
    train = train_grads.reshape(train_rows, features)

    bf16, f32 = jnp.bfloat16, jnp.float32
    dma = pltpu.SemaphoreType.DMA
    whole = 67043328
    smem = pl.BlockSpec(memory_space=pltpu.SMEM)
    words = pl.pallas_call(
        functools.partial(words_kernel, slots),
        out_shape=jax.ShapeDtypeStruct((NX,), jnp.int32),
        in_specs=[smem],
        out_specs=smem,
        name="words",
    )(pair_blocks)
    return pl.pallas_call(
        functools.partial(kernel, n_ex, layers, slots),
        out_shape=jax.ShapeDtypeStruct((1, slots, train_rows), f32),
        in_specs=[
            smem,
            smem,
            pl.BlockSpec(memory_space=pltpu.VMEM),
            pl.BlockSpec(memory_space=pltpu.VMEM),
            pl.BlockSpec(memory_space=pltpu.VMEM),
            pl.BlockSpec(memory_space=pl.ANY),
        ],
        out_specs=pl.BlockSpec(memory_space=pltpu.VMEM),
        scratch_shapes=[
            pltpu.VMEM((held_rows * features // LANES, LANES), f32),
            pltpu.VMEM((held_rows * features // LANES, LANES), f32),
            pltpu.VMEM((NC, held_rows, width), bf16),
            pltpu.VMEM((NC, held_rows, width), bf16),
            pltpu.VMEM((2 * items, held_rows, width), bf16),
            pltpu.VMEM((NC, ny, NX * rows, width), bf16),
            pltpu.VMEM((NC, ny, 3, rows, width), bf16),
            pltpu.VMEM((NC, ny, rows, width), bf16),
            pltpu.VMEM((NC, train_rows, width), bf16),
            pltpu.VMEM((cuts, ny * NX * rows, LANES), f32),
            pltpu.VMEM((half - 1, layers, cuts * 2 * NX, LANES), f32),
            pltpu.VMEM((half - 1, layers - 1, cuts * 2 * NX, LANES), f32),
            pltpu.VMEM((2, layers, cuts * NX, LANES), f32),
            pltpu.VMEM((2, layers - 1, cuts * NX, LANES), f32),
            pltpu.VMEM((ny * NX, train_rows), f32),
            dma((NC + 1,)),
            dma,
            dma((2 * items,)),
            dma,
            dma((NC, ny)),
            dma,
            dma((NC, ny)),
            dma,
            dma,
            dma((half - 1,)),
            dma((2,)),
        ],
        compiler_params=pltpu.CompilerParams(
            collective_id=0, has_side_effects=True, vmem_limit_bytes=whole
        ),
        name="tiles",
    )(words, pair_blocks, query, in_precond, out_precond, train)


def solution(mesh):
    in_specs = (
        P("ex", "layer", None),
        P("ex", "layer", None),
        P("layer", None, None),
        P("layer", None, None),
        P(),
    )
    out_specs = P("layer", "ex", None)
    return jax.shard_map(shards, mesh=mesh, in_specs=in_specs, out_specs=out_specs, check_vma=False)
```
